32 devices in a mesh: visit: 8 (over z, x), patch: 4 (over y, core).
Axes of the slice: x: 2, y: 2, z: 4, core: 2. Of those that a mesh axis runs over, the one named last changes fastest.
Arguments:
- tiles: bfloat16 [512, 128, 128], P(('visit', 'patch')), may hold values from -6 to 6
- tile_visit: int32 [512], P(('visit', 'patch')), may hold values from 0 to 24
- tile_variance: float32 [512], P(('visit', 'patch')), may hold values from 0.3 to 3
- intersection: int32 [512, 2], P(('visit', 'patch')), may hold values from 0 to 3, all different within a row; in each aligned block of 16 rows (0 to 15, 16 to 31, ...) at most 16 rows name the same one
- offsets: int32 [512, 2, 2], P(('visit', 'patch')), may hold values from -64 to 192
- extent: int32 [512, 2], P(('visit', 'patch')), may hold values from 64 to 128
- psf_coeffs: float32 [200, 27], P('visit'), may hold values from -3 to 3
Outputs:
- significance: float32 [4, 256, 256], P('patch', 'visit')
The draws below stay inside these ranges and needn't reach their ends.
Inputs may be any that keep to these rules, and one draw needn't show every extreme that they name: `intersection`: the two patches of a tile differ; among the 16 tiles of one device no patch is named by more than 16 entries, and every patch is named by some tile.
All inputs are finite; a program needn't handle non-finite values.
Results may differ from the reference program's by a relative error of at most 0.014.
Values may be sent and summed in bfloat16 or wider, within the bound.
A program may use at most 64 MiB of HBM per device.

```python
import math
import jax
import jax.numpy as jnp
import numpy as np
from jax import lax

TS = 128
PS = 256
HALF = 10
NBASIS = 27
T_DEV = 16
VIS_DEV = 25
PATCHES = 4
VISITS = 200
TILES = 512
CAP = 16
N_PATCH = 4


def plant(entries, own_key, low, high):
    spot = [jax.random.randint(jax.random.fold_in(own_key, axis), (), 0, length) for axis, length in enumerate(entries.shape)]
    main_axis = entries.shape.index(max(entries.shape))
    neighbour = spot[:main_axis] + [(spot[main_axis] + 1) % entries.shape[main_axis]] + spot[main_axis + 1:]
    return entries.at[tuple(spot)].set(low).at[tuple(neighbour)].set(high)


def steps_of(key, dims, pieces, low, top_value):
    loudness = 1.0
    for position, parts in pieces:
        heights = jax.random.uniform(jax.random.fold_in(jax.random.fold_in(key, 6), position), (parts,), jnp.float32, low / len(pieces), top_value / len(pieces))
        loudness = loudness * jnp.repeat(jnp.exp(heights), dims[position] // parts).reshape((-1,) + (1,) * (len(dims) - 1 - position))
    return loudness


def routed_block(rng, own, number, rows, amount, top, most, slope):
    order = jax.random.permutation(rng, amount)
    crowded, ordinary = portions_of(amount, rows * top, most, slope, True), portions_of(amount, rows * top, most, slope, False)
    places = jnp.arange(amount)

    def named(sizes, turn):
        used = int((sizes > 0).sum())
        fixed = max(1, used // 4)
        moved = fixed + (places - fixed + turn * (used - fixed)) % max(1, amount - fixed)
        return jnp.zeros((amount,), jnp.int32).at[order[jnp.where(places < fixed, places, moved)]].set(jnp.asarray(sizes, jnp.int32))

    sizes = jnp.where(number % 4 == 0, named(crowded, number // 4), named(ordinary, number - number // 4 - 1))
    mixed = jax.random.permutation(jax.random.fold_in(own, 3), amount)
    giver, taker = mixed[0:amount // 2 * 2:2], mixed[1:amount // 2 * 2:2]
    margin = jnp.minimum(sizes[giver] - 1, most - sizes[taker]) // 2
    margin = jnp.where((giver == order[0]) | (taker == order[0]) | (sizes[taker] == 0), 0, jnp.maximum(margin, 0))
    moved = jax.random.randint(jax.random.fold_in(own, 4), (amount // 2,), 0, 1 << 20) % (margin + 1)
    sizes = sizes.at[giver].add(-moved).at[taker].add(moved)
    items = jnp.searchsorted(jnp.cumsum(sizes), jnp.arange(rows * top), side="right").astype(jnp.int32)
    table = items.reshape(top, rows).T
    table = table[jax.random.permutation(jax.random.fold_in(own, 1), rows)]
    turn = jax.random.randint(jax.random.fold_in(own, 2), (rows, 1), 0, top)
    return jnp.take_along_axis(table, (jnp.arange(top)[None, :] + turn) % top, axis=1)


def portions_of(count, total, reach, slope, full):
    portions = [(1 << 20) // math.isqrt(grade ** slope) + 1 for grade in range(1, count + 1)]
    largest = reach if full else min(reach, max(-(-total // count), total * portions[0] // sum(portions)))
    least = 1 if total - largest >= count - 1 else 0
    counts, rest = [largest] + [least] * (count - 1), total - largest - least * (count - 1)
    while rest > 0:
        movable = [i for i in range(1, count) if counts[i] < largest] or [i for i in range(1, count) if counts[i] < reach]
        whole, remaining = sum([portions[i] for i in movable]), rest
        for i in movable:
            extra = min(reach - counts[i], max(1, remaining * portions[i] // whole), rest)
            counts[i] = counts[i] + extra
            rest = rest - extra
    return np.array(counts)


def noise(own_key, dims, spread, bound, shards=(), kind=jnp.bfloat16):
    values = spread * jax.random.normal(own_key, dims, jnp.float32)
    if shards:
        values = values * steps_of(own_key, dims, shards, -0.22, 0.18)
    return jnp.clip(values, -bound, bound).astype(kind)


def setup_inputs(seed: int = 0) -> dict:
    seeds = jax.random.split(jax.random.key(seed), 8)
    tiles = noise(seeds[0], (TILES, TS, TS), 1.0, 6.0, ((0, 32),))
    tile_visit = plant(jax.random.randint(seeds[1], (TILES,), 0, VIS_DEV), jax.random.fold_in(seeds[1], 1), 0, VIS_DEV - 1).astype(jnp.int32)
    tile_variance = jnp.clip(jnp.exp(math.log(3.0) - 2.3025851 * jax.random.uniform(seeds[2], (TILES,), jnp.float32) ** steps_of(seeds[2], (TILES,), ((0, 32),), -0.2, 0.2)), 0.3, 3.0)
    intersection_keys = jax.random.split(jax.random.fold_in(seeds[3], 1), TILES // T_DEV)
    intersection_turns = jax.random.permutation(jax.random.fold_in(seeds[3], 3), TILES // T_DEV)
    intersection = jax.vmap(lambda own, number: routed_block(jax.random.fold_in(seeds[3], 2), own, number, T_DEV, PATCHES, 2, CAP, 2))(intersection_keys, intersection_turns).reshape((TILES, 2))
    offsets = plant(jax.random.randint(seeds[4], (TILES, 2, 2), -(TS // 2), PS - TS // 2 + 1), jax.random.fold_in(seeds[4], 1), -(TS // 2), (PS - TS // 2 + 1) - 1).astype(jnp.int32)
    extent = plant(jax.random.randint(seeds[5], (TILES, 2), TS // 2, TS + 1), jax.random.fold_in(seeds[5], 1), TS // 2, TS).astype(jnp.int32)
    psf_coeffs = noise(seeds[6], (VISITS, NBASIS), 0.5, 3.0, ((0, 8),), jnp.float32)
    return {"tiles": tiles, "tile_visit": tile_visit, "tile_variance": tile_variance, "intersection": intersection, "offsets": offsets, "extent": extent, "psf_coeffs": psf_coeffs}


SIGMAS = (0.7, 1.5, 3.0)
HIGHEST = lax.Precision.HIGHEST

def basis_taps():
    lag_values = jnp.arange(2 * HALF + 1, dtype=jnp.float32) - float(HALF)
    groups = []
    for width_sigma in SIGMAS:
        scaled = lag_values / width_sigma
        gaussian = jnp.exp(-0.5 * scaled * scaled) / (math.sqrt(2.0 * math.pi) * width_sigma)
        groups.append(jnp.stack([gaussian, scaled * gaussian, scaled * scaled * gaussian]))
    return jnp.stack(groups)

def banded(tile_side):
    pixel_index = jnp.arange(tile_side, dtype=jnp.int32)
    lag_index = jnp.arange(2 * HALF + 1, dtype=jnp.int32) - HALF
    return (pixel_index[None, :, None] - pixel_index[None, None, :] == lag_index[:, None, None]).astype(jnp.float32)

def convolve(tile_block, coefficients, valid_size, weight):
    tile_side = tile_block.shape[-1]
    item_count = tile_block.shape[0]
    profiles = basis_taps()
    diagonal_band = banded(tile_side)
    x_filters = jnp.einsum('ku,uab->kab', profiles.reshape(9, -1), diagonal_band, precision=HIGHEST).astype(jnp.bfloat16)
    y_taps = jnp.einsum('nsij,sju->nsiu', coefficients.reshape(item_count, 3, 3, 3), profiles, precision=HIGHEST).reshape(item_count, 9, -1)
    flipped = jnp.swapaxes(diagonal_band, 1, 2)
    pixel_index = jnp.arange(tile_side, dtype=jnp.int32)
    inside = ((pixel_index[None, :, None] < valid_size[:, 0, None, None]) & (pixel_index[None, None, :] < valid_size[:, 1, None, None])).astype(jnp.bfloat16)
    masked = tile_block * inside
    summed = jnp.zeros((item_count, tile_side, tile_side), jnp.float32)
    for basis_term in range(9):
        y_filter = jnp.einsum('nu,udc->ndc', y_taps[:, basis_term], flipped, precision=HIGHEST).astype(jnp.bfloat16)
        smooth = jnp.einsum('nbd,ndc->nbc', masked.astype(jnp.float32), y_filter.astype(jnp.float32), precision=HIGHEST).astype(jnp.bfloat16)
        summed = summed + jnp.einsum('ab,nbc->nac', x_filters[basis_term].astype(jnp.float32), smooth.astype(jnp.float32), precision=HIGHEST)
    return (summed * weight[:, None, None] * inside.astype(jnp.float32)).astype(jnp.bfloat16)

def reference(tiles, tile_visit, tile_variance, intersection, offsets, extent, psf_coeffs):
    tile_index = jnp.arange(TILES, dtype=jnp.int32)
    visit_row = tile_index // (T_DEV * N_PATCH) * VIS_DEV + tile_visit.astype(jnp.int32)
    coefficients = psf_coeffs[visit_row]
    weight = 1.0 / tile_variance
    blocks = TILES // T_DEV

    def match_block(packed):
        block_tiles, block_coeff, block_extent, block_weight = packed
        return convolve(block_tiles, block_coeff, block_extent, block_weight)
    weighted = lax.map(match_block, (tiles.reshape(blocks, T_DEV, TS, TS), coefficients.reshape(blocks, T_DEV, -1), extent.reshape(blocks, T_DEV, 2), weight.reshape(blocks, T_DEV))).reshape(TILES, TS, TS)
    canvas_side = PS + 2 * TS

    def place(carry, packed):
        numerator, denominator = carry
        matched, patches, shifts, valid_size, tile_weight = packed
        pixel_index = jnp.arange(TS, dtype=jnp.int32)
        inside = ((pixel_index[:, None] < valid_size[0]) & (pixel_index[None, :] < valid_size[1])).astype(jnp.float32)
        for intersection_slot in range(2):
            corner = (patches[intersection_slot].astype(jnp.int32), (shifts[intersection_slot, 0] + TS).astype(jnp.int32), (shifts[intersection_slot, 1] + TS).astype(jnp.int32))
            numerator = lax.dynamic_update_slice(numerator, lax.dynamic_slice(numerator, corner, (1, TS, TS)) + matched.astype(jnp.float32)[None], corner)
            denominator = lax.dynamic_update_slice(denominator, lax.dynamic_slice(denominator, corner, (1, TS, TS)) + (tile_weight * inside)[None], corner)
        return ((numerator, denominator), None)
    blank_canvas = jnp.zeros((N_PATCH, canvas_side, canvas_side), jnp.float32)
    (numerator, denominator), unused = lax.scan(place, (blank_canvas, blank_canvas), (weighted, intersection, offsets, extent, weight))
    numerator = numerator[:, TS:TS + PS, TS:TS + PS]
    denominator = denominator[:, TS:TS + PS, TS:TS + PS]
    return numerator / jnp.sqrt(denominator + 1.0)
```

```python
import functools
import math

import jax
import jax.numpy as jnp
import numpy as np
from jax import lax
from jax.experimental import pallas as pl
from jax.experimental.pallas import tpu as pltpu
from jax.sharding import PartitionSpec as P

PS = 256
HALF = 10
SIGMAS = (0.7, 1.5, 3.0)
MESH = pl.DeviceIdType.MESH
F32, BF16 = jnp.float32, jnp.bfloat16


def taps():
    lag = np.arange(-HALF, HALF + 1, dtype=np.float32)
    rows = []
    for sigma in SIGMAS:
        scaled = (lag / np.float32(sigma)).astype(np.float32)
        gaussian = np.exp(np.float32(-0.5) * scaled * scaled) / np.float32(
            math.sqrt(2.0 * math.pi) * sigma
        )
        rows += [gaussian, scaled * gaussian, scaled * scaled * gaussian]
    return np.stack(rows).astype(np.float32)


def filters(side):
    pixel = np.arange(side)
    lag = pixel[:, None] - pixel[None, :]
    banded = np.where(
        np.abs(lag) <= HALF, taps()[:, np.clip(lag, -HALF, HALF) + HALF], np.float32(0)
    )
    x_filter = np.concatenate(list(banded), axis=1)
    stagger = np.zeros((9, 16, side), np.float32)
    for i in range(16):
        stagger[:, i, i:i + 2 * HALF + 1] = taps()
    return x_filter, stagger


def repeat(count, step):
    if count <= 8:
        for i in range(count):
            step(i)
    else:
        def body(i, carry):
            step(i)
            return carry

        lax.fori_loop(0, count, body, 0)


def kernel(dims, *refs):
    inputs, (flux_ref, depth_ref), held, rest = refs[:9], refs[9:11], refs[11:20], refs[20:]
    work(dims, inputs, held, flux_ref, depth_ref, *rest)


def work(
    dims, inputs, held, flux_ref, depth_ref, load_sem,
    matched, away, from_pair, ready, landed, meta_own, meta_pair,
    pair_send, pair_recv, mp_sem, send_sem, recv_sem,
):
    n_visit, n_patch, tile_count, side = dims
    visit_ref, variance_ref, inter_ref, offset_ref, extent_ref, psf_ref, tiles_ref, x_ref, g_ref = held
    loads = [pltpu.make_async_copy(a, b, load_sem.at[i]) for i, (a, b) in enumerate(zip(inputs, held))]
    for load in loads:
        load.start()
    n_y = n_patch // 2
    rows = PS // n_visit
    slots = n_visit * n_y
    v = lax.axis_index("visit")
    p = lax.axis_index("patch")
    core = lax.rem(p, 2)
    chip_y = lax.div(p, 2)
    pair = (v, p + 1 - 2 * core)

    def target(k):
        return (lax.rem(v + lax.rem(k, n_visit), n_visit), lax.rem(chip_y + lax.div(k, n_visit), n_y))

    barrier = pltpu.get_barrier_semaphore()
    pl.semaphore_signal(barrier, inc=1, device_id=pair, device_id_type=MESH)

    def greet(k, carry):
        tv, ty = target(k)
        pl.semaphore_signal(barrier, inc=1, device_id=(tv, 2 * ty + core), device_id_type=MESH)
        return carry

    lax.fori_loop(1, slots, greet, 0)
    for load in loads:
        load.wait()

    field = lax.broadcasted_iota(jnp.int32, (16, 128), 0)
    lane = lax.broadcasted_iota(jnp.int32, (16, 128), 1)
    table = jnp.zeros((16, 128), F32)
    for t in range(tile_count):
        for k in range(2):
            scalars = (inter_ref[k, t], offset_ref[k, 0, t], offset_ref[k, 1, t],
                       extent_ref[0, t], extent_ref[1, t])
            column = jnp.full((16, 128), variance_ref[t], F32)
            for f, value in enumerate(scalars):
                column = jnp.where(field == f, value.astype(F32), column)
            table = jnp.where(lane == 2 * tile_count * core + 2 * t + k, column, table)
    used = (lane >= 2 * tile_count * core) & (lane < 2 * tile_count * (core + 1))
    inverse = jnp.where(used, 1.0 / jnp.where(used, table, 1.0), 0.0)
    coarse = inverse.astype(BF16).astype(F32)
    table = jnp.where(field == 5, coarse, jnp.where(field == 6, inverse - coarse, table))
    table = jnp.where(field > 6, 0.0, table)
    meta_own[...] = table.astype(BF16)

    row_of = lax.broadcasted_iota(jnp.int32, (side, side), 0)
    col_of = lax.broadcasted_iota(jnp.int32, (side, side), 1)
    row_gap = (
        lax.broadcasted_iota(jnp.int32, (PS, side), 0)
        - lax.broadcasted_iota(jnp.int32, (PS, side), 1)
    ).astype(F32).astype(BF16)
    one, zero = jnp.ones((), BF16), jnp.zeros((), BF16)
    left_part = lane < side // 2

    def y_filter(t, s, d):
        c = [psf_ref[visit_ref[t], 9 * s + 3 * d + j] for j in range(3)]
        row = c[0] * g_ref[3 * s] + c[1] * g_ref[3 * s + 1] + c[2] * g_ref[3 * s + 2]
        row = row.astype(BF16)
        blocks = []
        for b in range(side // 16):
            block = pltpu.roll(row, (16 * b - HALF) % side, 1)
            if b == 0:
                block = jnp.where(left_part, block, zero)
            elif b == side // 16 - 1:
                block = jnp.where(left_part, zero, block)
            blocks.append(block)
        return jnp.concatenate(blocks, axis=0)

    def match(i):
        halves = (2 * i, 2 * i + 1)
        inside = [(row_of < extent_ref[0, t]) & (col_of < extent_ref[1, t]) for t in halves]
        stacked = []
        for t, m in zip(halves, inside):
            masked = jnp.where(m, tiles_ref[t].astype(F32), 0.0).astype(BF16)
            wide = jnp.concatenate([y_filter(t, s, d) for s in range(3) for d in range(3)], axis=1)
            smooth = jnp.dot(masked, wide, preferred_element_type=F32).astype(BF16)
            stacked.append(
                jnp.concatenate([smooth[:, side * b:side * (b + 1)] for b in range(9)], axis=0)
            )
        convolved = jnp.dot(
            x_ref[...], jnp.concatenate(stacked, axis=1), preferred_element_type=F32
        )
        for h, t in enumerate(halves):
            scale = 1.0 / jnp.full((8, side), variance_ref[t], F32)
            matched[t] = jnp.where(
                inside[h], convolved[:, side * h:side * (h + 1)] * scale[0:1], 0.0
            ).astype(BF16)

    for i in range(tile_count // 2):
        match(i)

    def patch_sum(number):
        chosen, blocks = [], []
        for t in range(tile_count):
            first, second = inter_ref[0, t] == number, inter_ref[1, t] == number
            shift = jnp.where(
                first, offset_ref[0, 0, t], jnp.where(second, offset_ref[1, 0, t], 1024)
            )
            shift = jnp.full((PS, side), shift.astype(F32), F32).astype(BF16)
            chosen.append(jnp.where(row_gap == shift, one, zero))
            column = jnp.where(first, offset_ref[0, 1, t], offset_ref[1, 1, t])
            turned = pltpu.roll(matched[t], jnp.bitwise_and(column, side - 1), 1)
            gap = lane - column
            halves = []
            for low in (0, -side):
                mask = jnp.where((gap >= low) & (gap < low + side), 1.0, 0.0).astype(BF16)
                halves.append(turned * jnp.concatenate([mask] * (side // 16), axis=0))
            blocks.append(jnp.concatenate(halves, axis=1))
        return jnp.dot(
            jnp.concatenate(chosen, axis=1), jnp.concatenate(blocks, axis=0),
            preferred_element_type=F32,
        ).reshape(n_visit, rows, PS)

    def pair_copy(y):
        return pltpu.make_async_remote_copy(
            src_ref=away.at[y], dst_ref=from_pair.at[y],
            send_sem=pair_send.at[y], recv_sem=pair_recv.at[y],
            device_id=pair, device_id_type=MESH,
        )

    meta_copy = pltpu.make_async_remote_copy(
        src_ref=meta_own, dst_ref=meta_pair, send_sem=mp_sem.at[0], recv_sem=mp_sem.at[1],
        device_id=pair, device_id_type=MESH,
    )

    def give(y):
        away[y] = patch_sum(2 * y + 1 - core).astype(BF16)

    give(0)
    pl.semaphore_wait(barrier, slots)
    pair_copy(0).start()
    meta_copy.start()

    def give_next(y):
        give(y + 1)
        pair_copy(y + 1).start()

    repeat(n_y - 1, give_next)
    meta_copy.wait()
    meta = meta_own[...].astype(F32) + meta_pair[...].astype(F32)

    def slot_of(dv, dy):
        return lax.rem(dy + n_y, n_y) * n_visit + lax.rem(dv + n_visit, n_visit)

    def block_to(k):
        tv, ty = target(k)
        return pltpu.make_async_remote_copy(
            src_ref=ready.at[ty, tv], dst_ref=landed.at[k],
            send_sem=send_sem.at[k], recv_sem=recv_sem.at[k],
            device_id=(tv, 2 * ty + core), device_id_type=MESH,
        )

    def keep(y):
        total = patch_sum(2 * y + core)
        pair_copy(y).wait()
        total = total + from_pair[y].astype(F32)
        ready[y] = jnp.concatenate(
            [total[:, :, :128], total[:, :, 128:],
             jnp.broadcast_to(meta[None], (n_visit, 16, 128))], axis=1,
        ).astype(BF16)

        def send(tv):
            k = slot_of(tv - v, y - chip_y)

            @pl.when(k > 0)
            def _():
                block_to(k).start()

        repeat(n_visit, send)

    repeat(n_y, keep)

    canvas_row = (lax.broadcasted_iota(jnp.int32, (rows, 128), 0) + v * rows).astype(F32)
    canvas_col = lax.broadcasted_iota(jnp.int32, (PS, 128), 0).astype(F32)
    mine = p.astype(F32)

    def weigh(meta):
        here = meta[0:1] == mine
        in_row = (canvas_row >= meta[1:2]) & (canvas_row < meta[1:2] + meta[3:4])
        in_col = (canvas_col >= meta[2:3]) & (canvas_col < meta[2:3] + meta[4:5])
        high = jnp.where(in_row, jnp.where(here, meta[5:6], 0.0), 0.0)
        low = jnp.where(in_row, jnp.where(here, meta[6:7], 0.0), 0.0)
        both = lax.dot_general(
            jnp.concatenate([high, low], axis=0).astype(BF16),
            jnp.where(in_col, 1.0, 0.0).astype(BF16),
            (((1,), (1,)), ((), ())), preferred_element_type=F32,
        )
        return both[:rows] + both[rows:]

    def add(block, left, right, depth):
        block = block.astype(F32)
        return (left + block[:rows], right + block[rows:2 * rows],
                depth + weigh(block[2 * rows:]))

    here = v * n_y + chip_y

    def arrive(i, carry):
        source = i + jnp.where(i >= here, 1, 0)
        k = slot_of(v - lax.div(source, n_y), chip_y - lax.rem(source, n_y))
        block_to(k).wait()
        return add(landed[k], *carry)

    blank = jnp.zeros((rows, 128), F32)
    carry = add(ready[chip_y, v], blank, blank, jnp.zeros((rows, PS), F32))
    left, right, depth = lax.fori_loop(0, slots - 1, arrive, carry)
    flux_ref[:, :128] = left
    flux_ref[:, 128:] = right
    depth_ref[...] = depth


def solution(mesh):
    n_visit, n_patch = mesh.shape["visit"], mesh.shape["patch"]

    def body(tiles, tile_visit, tile_variance, intersection, offsets, extent, psf_coeffs):
        tile_count, side = tiles.shape[0], tiles.shape[1]
        rows = PS // n_visit
        n_y = n_patch // 2
        slots = n_visit * n_y
        x_filter, stagger = filters(side)
        anywhere = pl.BlockSpec(memory_space=pl.ANY)
        arrays = (
            tile_visit, tile_variance, intersection.T, jnp.transpose(offsets, (1, 2, 0)), extent.T,
            psf_coeffs, tiles, jnp.asarray(x_filter, BF16), jnp.asarray(stagger, F32),
        )
        vmem = pl.BlockSpec(memory_space=pltpu.VMEM)
        dma = pltpu.SemaphoreType.DMA
        flux, depth = pl.pallas_call(
            functools.partial(kernel, (n_visit, n_patch, tile_count, side)),
            out_shape=[pltpu.VMEM((rows, PS), F32)] * 2,
            in_specs=[anywhere] * 9,
            out_specs=[vmem] * 2,
            scratch_shapes=[pltpu.SMEM(a.shape, a.dtype) for a in arrays[:6]]
            + [pltpu.VMEM(a.shape, a.dtype) for a in arrays[6:]]
            + [
                dma((9,)),
                pltpu.VMEM((tile_count, side, side), BF16),
                pltpu.VMEM((n_y, n_visit, rows, PS), BF16),
                pltpu.VMEM((n_y, n_visit, rows, PS), BF16),
                pltpu.VMEM((n_y, n_visit, 2 * rows + 16, 128), BF16),
                pltpu.VMEM((slots, 2 * rows + 16, 128), BF16),
                pltpu.VMEM((16, 128), BF16),
                pltpu.VMEM((16, 128), BF16),
                dma((n_y,)), dma((n_y,)), dma((2,)),
                dma((slots,)), dma((slots,)),
            ],
            compiler_params=pltpu.CompilerParams(
                collective_id=0, has_side_effects=True, vmem_limit_bytes=62 * 2**20
            ),
        )(*[pltpu.with_memory_space_constraint(a, pltpu.HBM) for a in arrays])
        return (flux / jnp.sqrt(depth + 1.0))[None]

    return jax.shard_map(
        body,
        mesh=mesh,
        in_specs=(
            P(("visit", "patch"), None, None),
            P(("visit", "patch")),
            P(("visit", "patch")),
            P(("visit", "patch"), None),
            P(("visit", "patch"), None, None),
            P(("visit", "patch"), None),
            P("visit", None),
        ),
        out_specs=P("patch", "visit", None),
        check_vma=False,
    )
```

```python
import functools
import math

import jax
import jax.numpy as jnp
import numpy as np
from jax import lax
from jax.experimental import pallas as pl
from jax.experimental.pallas import tpu as pltpu
from jax.sharding import PartitionSpec as P

PS = 256
HALF = 10
SIGMAS = (0.7, 1.5, 3.0)
MESH = pl.DeviceIdType.MESH
F32, BF16 = jnp.float32, jnp.bfloat16


def taps():
    lag = np.arange(-HALF, HALF + 1, dtype=np.float32)
    rows = []
    for sigma in SIGMAS:
        scaled = (lag / np.float32(sigma)).astype(np.float32)
        gaussian = np.exp(np.float32(-0.5) * scaled * scaled) / np.float32(
            math.sqrt(2.0 * math.pi) * sigma
        )
        rows += [gaussian, scaled * gaussian, scaled * scaled * gaussian]
    return np.stack(rows).astype(np.float32)


def filters(side):
    pixel = np.arange(side)
    lag = pixel[:, None] - pixel[None, :]
    banded = np.where(
        np.abs(lag) <= HALF, taps()[:, np.clip(lag, -HALF, HALF) + HALF], np.float32(0)
    )
    x_filter = np.concatenate(list(banded), axis=1)
    stagger = np.zeros((9, 16, side), np.float32)
    for i in range(16):
        stagger[:, i, i:i + 2 * HALF + 1] = taps()
    return x_filter, stagger


def repeat(count, step):
    if count <= 16:
        for i in range(count):
            step(i)
    else:
        def body(i, carry):
            step(i)
            return carry

        lax.fori_loop(0, count, body, 0)


def kernel(dims, *refs):
    inputs, (flux_ref, depth_ref), held, rest = refs[:9], refs[9:11], refs[11:20], refs[20:]
    work(dims, inputs, held, flux_ref, depth_ref, *rest)


def work(
    dims, inputs, held, flux_ref, depth_ref, load_sem,
    matched, away, from_pair, ready, landed, meta_own, meta_pair, meta_ready, meta_landed,
    pair_send, pair_recv, mp_sem, send_sem, recv_sem, msend_sem, mrecv_sem,
):
    n_visit, n_patch, tile_count, side = dims
    visit_ref, variance_ref, inter_ref, offset_ref, extent_ref, psf_ref, tiles_ref, x_ref, g_ref = held
    loads = [pltpu.make_async_copy(a, b, load_sem.at[i]) for i, (a, b) in enumerate(zip(inputs, held))]
    for load in loads:
        load.start()
    n_y = n_patch // 2
    rows = PS // n_visit
    slots = n_visit * n_y
    v = lax.axis_index("visit")
    p = lax.axis_index("patch")
    core = lax.rem(p, 2)
    chip_y = lax.div(p, 2)
    pair = (v, p + 1 - 2 * core)

    def target(k):
        return (lax.rem(v + lax.rem(k, n_visit), n_visit), lax.rem(chip_y + lax.div(k, n_visit), n_y))

    barrier = pltpu.get_barrier_semaphore()
    pl.semaphore_signal(barrier, inc=1, device_id=pair, device_id_type=MESH)

    def greet(k, carry):
        tv, ty = target(k)
        pl.semaphore_signal(barrier, inc=1, device_id=(tv, 2 * ty + core), device_id_type=MESH)
        return carry

    lax.fori_loop(1, slots, greet, 0)
    for load in loads:
        load.wait()

    field = lax.broadcasted_iota(jnp.int32, (4, 128), 0)
    entry = lax.broadcasted_iota(jnp.int32, (4, 128), 1)
    table = jnp.zeros((4, 128), F32)
    at = 2 * tile_count * core
    for t in range(tile_count):
        size = jnp.where(
            field == 0, extent_ref[0, t].astype(F32),
            jnp.where(field == 1, extent_ref[1, t].astype(F32), variance_ref[t]),
        )
        for k in range(2):
            spot = jnp.where(
                field == 0, inter_ref[k, t].astype(F32),
                jnp.where(field == 1, offset_ref[k, 0, t].astype(F32), offset_ref[k, 1, t].astype(F32)),
            )
            table = jnp.where(entry == at + 2 * t + k, spot, table)
            table = jnp.where(entry == at + 64 + 2 * t + k, size, table)
    own_size = (field == 2) & (entry >= at + 64) & (entry < at + 64 + 2 * tile_count)
    meta_own[...] = jnp.where(own_size, 1.0 / jnp.where(own_size, table, 1.0), table)

    row_of = lax.broadcasted_iota(jnp.int32, (side, side), 0)
    col_of = lax.broadcasted_iota(jnp.int32, (side, side), 1)
    row_gap = (
        lax.broadcasted_iota(jnp.int32, (PS, side), 0)
        - lax.broadcasted_iota(jnp.int32, (PS, side), 1)
    ).astype(F32).astype(BF16)
    one, zero = jnp.ones((), BF16), jnp.zeros((), BF16)
    lane = lax.broadcasted_iota(jnp.int32, (16, 128), 1)
    left_part = lane < side // 2

    def y_filter(t, s, d):
        c = [psf_ref[visit_ref[t], 9 * s + 3 * d + j] for j in range(3)]
        row = c[0] * g_ref[3 * s] + c[1] * g_ref[3 * s + 1] + c[2] * g_ref[3 * s + 2]
        row = row.astype(BF16)
        blocks = []
        for b in range(side // 16):
            block = pltpu.roll(row, (16 * b - HALF) % side, 1)
            if b == 0:
                block = jnp.where(left_part, block, zero)
            elif b == side // 16 - 1:
                block = jnp.where(left_part, zero, block)
            blocks.append(block)
        return jnp.concatenate(blocks, axis=0)

    def match(i):
        halves = (2 * i, 2 * i + 1)
        inside = [(row_of < extent_ref[0, t]) & (col_of < extent_ref[1, t]) for t in halves]
        stacked = []
        for t, m in zip(halves, inside):
            masked = jnp.where(m, tiles_ref[t].astype(F32), 0.0).astype(BF16)
            wide = jnp.concatenate([y_filter(t, s, d) for s in range(3) for d in range(3)], axis=1)
            smooth = jnp.dot(masked, wide, preferred_element_type=F32).astype(BF16)
            stacked.append(
                jnp.concatenate([smooth[:, side * b:side * (b + 1)] for b in range(9)], axis=0)
            )
        convolved = jnp.dot(
            x_ref[...], jnp.concatenate(stacked, axis=1), preferred_element_type=F32
        )
        for h, t in enumerate(halves):
            scale = 1.0 / jnp.full((8, side), variance_ref[t], F32)
            matched[t] = jnp.where(
                inside[h], convolved[:, side * h:side * (h + 1)] * scale[0:1], 0.0
            ).astype(BF16)

    for i in range(tile_count // 2):
        match(i)

    def patch_sum(number):
        chosen, blocks = [], []
        for t in range(tile_count):
            first, second = inter_ref[0, t] == number, inter_ref[1, t] == number
            shift = jnp.where(
                first, offset_ref[0, 0, t], jnp.where(second, offset_ref[1, 0, t], 1024)
            )
            shift = jnp.full((PS, side), shift.astype(F32), F32).astype(BF16)
            chosen.append(jnp.where(row_gap == shift, one, zero))
            column = jnp.where(first, offset_ref[0, 1, t], offset_ref[1, 1, t])
            turned = pltpu.roll(matched[t], jnp.bitwise_and(column, side - 1), 1)
            gap = lane - column
            halves = []
            for low in (0, -side):
                mask = jnp.where((gap >= low) & (gap < low + side), 1.0, 0.0).astype(BF16)
                halves.append(turned * jnp.concatenate([mask] * (side // 16), axis=0))
            blocks.append(jnp.concatenate(halves, axis=1))
        return jnp.dot(
            jnp.concatenate(chosen, axis=1), jnp.concatenate(blocks, axis=0),
            preferred_element_type=F32,
        ).reshape(n_visit, rows, PS)

    def pair_copy(y):
        return pltpu.make_async_remote_copy(
            src_ref=away.at[y], dst_ref=from_pair.at[y],
            send_sem=pair_send.at[y], recv_sem=pair_recv.at[y],
            device_id=pair, device_id_type=MESH,
        )

    meta_copy = pltpu.make_async_remote_copy(
        src_ref=meta_own, dst_ref=meta_pair, send_sem=mp_sem.at[0], recv_sem=mp_sem.at[1],
        device_id=pair, device_id_type=MESH,
    )

    def give(y):
        away[y] = patch_sum(2 * y + 1 - core).astype(BF16)

    def slot_of(dv, dy):
        return lax.rem(dy + n_y, n_y) * n_visit + lax.rem(dv + n_visit, n_visit)

    def meta_to(k):
        tv, ty = target(k)
        return pltpu.make_async_remote_copy(
            src_ref=meta_ready, dst_ref=meta_landed.at[k],
            send_sem=msend_sem.at[k], recv_sem=mrecv_sem.at[k],
            device_id=(tv, 2 * ty + core), device_id_type=MESH,
        )

    def block_to(k):
        tv, ty = target(k)
        return pltpu.make_async_remote_copy(
            src_ref=ready.at[ty, tv], dst_ref=landed.at[k],
            send_sem=send_sem.at[k], recv_sem=recv_sem.at[k],
            device_id=(tv, 2 * ty + core), device_id_type=MESH,
        )

    give(0)
    pl.semaphore_wait(barrier, slots)
    meta_copy.start()
    pair_copy(0).start()

    def give_next(y):
        give(y + 1)
        pair_copy(y + 1).start()

    repeat(n_y - 1, give_next)
    meta_copy.wait()
    meta_ready[...] = meta_own[...] + meta_pair[...]
    repeat(slots - 1, lambda i: meta_to(i + 1).start())

    def keep(y):
        total = patch_sum(2 * y + core)
        pair_copy(y).wait()
        ready[y] = (total + from_pair[y].astype(F32)).astype(BF16)

    ORDER = sorted(
        [(tv, ty) for ty in range(n_y) for tv in range(n_visit)],
        key=lambda a: (a[0] // 2 + a[0] % 2 + a[1], a[1]),
    )
    own = sum(jnp.where((v == tv) & (chip_y == ty), j, 0) for j, (tv, ty) in enumerate(ORDER)) if slots <= 16 else 0

    def send(i):
        if slots <= 16:
            tv = jnp.where(i >= own, ORDER[i + 1][0], ORDER[i][0])
            ty = jnp.where(i >= own, ORDER[i + 1][1], ORDER[i][1])
            block_to(slot_of(tv - v, ty - chip_y)).start()
        else:
            block_to(i + 1).start()

    early = 2 if n_y == 2 else 0
    keep(0)
    repeat(early, send)
    repeat(n_y - 1, lambda y: keep(y + 1))
    repeat(slots - 1 - early, lambda i: send(i + early))

    canvas_row = (lax.broadcasted_iota(jnp.int32, (rows, 128), 0) + v * rows).astype(F32)
    canvas_col = lax.broadcasted_iota(jnp.int32, (PS, 128), 0).astype(F32)
    mine = p.astype(F32)
    first_half = entry < 64

    def weigh(one_chip, other_chip):
        spot = jnp.where(first_half, one_chip, pltpu.roll(other_chip, 64, 1))
        size = jnp.where(first_half, pltpu.roll(one_chip, 64, 1), other_chip)
        in_row = (canvas_row >= spot[1:2]) & (canvas_row < spot[1:2] + size[0:1])
        in_col = (canvas_col >= spot[2:3]) & (canvas_col < spot[2:3] + size[1:2])
        weight = jnp.where(spot[0:1] == mine, size[2:3], 0.0)
        coarse = weight.astype(BF16).astype(F32)
        both = lax.dot_general(
            jnp.concatenate(
                [jnp.where(in_row, coarse, 0.0), jnp.where(in_row, weight - coarse, 0.0)], axis=0
            ).astype(BF16),
            jnp.where(in_col, 1.0, 0.0).astype(BF16),
            (((1,), (1,)), ((), ())), preferred_element_type=F32,
        )
        return both[:rows] + both[rows:]

    def add_meta(i, depth):
        meta_to(2 * i).wait()
        meta_to(2 * i + 1).wait()
        return depth + weigh(meta_landed[2 * i], meta_landed[2 * i + 1])

    meta_to(1).wait()
    depth_ref[...] = lax.fori_loop(1, slots // 2, add_meta, weigh(meta_ready[...], meta_landed[1]))

    here = v * n_y + chip_y

    def add_block(i, total):
        source = i + jnp.where(i >= here, 1, 0)
        k = slot_of(v - lax.div(source, n_y), chip_y - lax.rem(source, n_y))
        block_to(k).wait()
        return total + landed[k].astype(F32)

    flux_ref[...] = lax.fori_loop(0, slots - 1, add_block, ready[chip_y, v].astype(F32))


def solution(mesh):
    n_visit, n_patch = mesh.shape["visit"], mesh.shape["patch"]

    def body(tiles, tile_visit, tile_variance, intersection, offsets, extent, psf_coeffs):
        tile_count, side = tiles.shape[0], tiles.shape[1]
        rows = PS // n_visit
        n_y = n_patch // 2
        slots = n_visit * n_y
        x_filter, stagger = filters(side)
        anywhere = pl.BlockSpec(memory_space=pl.ANY)
        arrays = (
            tile_visit, tile_variance, intersection.T, jnp.transpose(offsets, (1, 2, 0)), extent.T,
            psf_coeffs, tiles, jnp.asarray(x_filter, BF16), jnp.asarray(stagger, F32),
        )
        vmem = pl.BlockSpec(memory_space=pltpu.VMEM)
        dma = pltpu.SemaphoreType.DMA
        flux, depth = pl.pallas_call(
            functools.partial(kernel, (n_visit, n_patch, tile_count, side)),
            out_shape=[pltpu.VMEM((rows, PS), F32)] * 2,
            in_specs=[anywhere] * 9,
            out_specs=[vmem] * 2,
            scratch_shapes=[pltpu.SMEM(a.shape, a.dtype) for a in arrays[:6]]
            + [pltpu.VMEM(a.shape, a.dtype) for a in arrays[6:]]
            + [
                dma((9,)),
                pltpu.VMEM((tile_count, side, side), BF16),
                pltpu.VMEM((n_y, n_visit, rows, PS), BF16),
                pltpu.VMEM((n_y, n_visit, rows, PS), BF16),
                pltpu.VMEM((n_y, n_visit, rows, PS), BF16),
                pltpu.VMEM((slots, rows, PS), BF16),
                pltpu.VMEM((4, 128), F32),
                pltpu.VMEM((4, 128), F32),
                pltpu.VMEM((4, 128), F32),
                pltpu.VMEM((slots, 4, 128), F32),
                dma((n_y,)), dma((n_y,)), dma((2,)),
                dma((slots,)), dma((slots,)), dma((slots,)), dma((slots,)),
            ],
            compiler_params=pltpu.CompilerParams(
                collective_id=0, has_side_effects=True, vmem_limit_bytes=62 * 2**20
            ),
        )(*[pltpu.with_memory_space_constraint(a, pltpu.HBM) for a in arrays])
        return (flux / jnp.sqrt(depth + 1.0))[None]

    return jax.shard_map(
        body,
        mesh=mesh,
        in_specs=(
            P(("visit", "patch"), None, None),
            P(("visit", "patch")),
            P(("visit", "patch")),
            P(("visit", "patch"), None),
            P(("visit", "patch"), None, None),
            P(("visit", "patch"), None),
            P("visit", None),
        ),
        out_specs=P("patch", "visit", None),
        check_vma=False,
    )
```

```python
import functools
import math

import jax
import jax.numpy as jnp
import numpy as np
from jax import lax
from jax.experimental import pallas as pl
from jax.experimental.pallas import tpu as pltpu
from jax.sharding import PartitionSpec as P

PS = 256
HALF = 10
SIGMAS = (0.7, 1.5, 3.0)
MESH = pl.DeviceIdType.MESH
F32, BF16 = jnp.float32, jnp.bfloat16


def taps():
    lag = np.arange(-HALF, HALF + 1, dtype=np.float32)
    rows = []
    for sigma in SIGMAS:
        scaled = (lag / np.float32(sigma)).astype(np.float32)
        gaussian = np.exp(np.float32(-0.5) * scaled * scaled) / np.float32(
            math.sqrt(2.0 * math.pi) * sigma
        )
        rows += [gaussian, scaled * gaussian, scaled * scaled * gaussian]
    return np.stack(rows).astype(np.float32)


def filters(side):
    pixel = np.arange(side)
    lag = pixel[:, None] - pixel[None, :]
    banded = np.where(
        np.abs(lag) <= HALF, taps()[:, np.clip(lag, -HALF, HALF) + HALF], np.float32(0)
    )
    x_filter = np.concatenate(list(banded), axis=1)
    stagger = np.zeros((9, 16, side), np.float32)
    for i in range(16):
        stagger[:, i, i:i + 2 * HALF + 1] = taps()
    return x_filter, stagger


def repeat(count, step):
    if count <= 16:
        for i in range(count):
            step(i)
    else:
        def body(i, carry):
            step(i)
            return carry

        lax.fori_loop(0, count, body, 0)


def kernel(dims, *refs):
    inputs, (flux_ref, depth_ref), held, rest = refs[:9], refs[9:11], refs[11:20], refs[20:]
    work(dims, inputs, held, flux_ref, depth_ref, *rest)


def work(
    dims, inputs, held, flux_ref, depth_ref, load_sem,
    matched, away, from_pair, ready, landed, meta_own, meta_pair, meta_ready, meta_landed,
    pair_send, pair_recv, mp_send, mp_recv, send_sem, recv_sem, msend_sem, mrecv_sem,
):
    n_visit, n_patch, tile_count, side = dims
    visit_ref, variance_ref, inter_ref, offset_ref, extent_ref, psf_ref, tiles_ref, x_ref, g_ref = held
    loads = [pltpu.make_async_copy(a, b, load_sem.at[i]) for i, (a, b) in enumerate(zip(inputs, held))]
    for load in loads:
        load.start()
    n_y = n_patch // 2
    rows = PS // n_visit
    slots = n_visit * n_y
    v = lax.axis_index("visit")
    p = lax.axis_index("patch")
    core = lax.rem(p, 2)
    chip_y = lax.div(p, 2)
    pair = (v, p + 1 - 2 * core)

    def target(k):
        return (lax.rem(v + lax.rem(k, n_visit), n_visit), lax.rem(chip_y + lax.div(k, n_visit), n_y))

    barrier = pltpu.get_barrier_semaphore()
    pl.semaphore_signal(barrier, inc=1, device_id=pair, device_id_type=MESH)

    def greet(k, carry):
        tv, ty = target(k)
        pl.semaphore_signal(barrier, inc=1, device_id=(tv, 2 * ty + core), device_id_type=MESH)
        return carry

    lax.fori_loop(1, slots, greet, 0)
    for load in loads:
        load.wait()

    field = lax.broadcasted_iota(jnp.int32, (4, 128), 0)
    entry = lax.broadcasted_iota(jnp.int32, (4, 128), 1)
    table = jnp.zeros((4, 128), F32)
    at = 2 * tile_count * core
    for t in range(tile_count):
        size = jnp.where(
            field == 0, extent_ref[0, t].astype(F32),
            jnp.where(field == 1, extent_ref[1, t].astype(F32), variance_ref[t]),
        )
        for k in range(2):
            spot = jnp.where(
                field == 0, inter_ref[k, t].astype(F32),
                jnp.where(field == 1, offset_ref[k, 0, t].astype(F32), offset_ref[k, 1, t].astype(F32)),
            )
            table = jnp.where(entry == at + 2 * t + k, spot, table)
            table = jnp.where(entry == at + 64 + 2 * t + k, size, table)
    own_size = (field == 2) & (entry >= at + 64) & (entry < at + 64 + 2 * tile_count)
    meta_own[...] = jnp.where(own_size, 1.0 / jnp.where(own_size, table, 1.0), table)

    row_of = lax.broadcasted_iota(jnp.int32, (side, side), 0)
    col_of = lax.broadcasted_iota(jnp.int32, (side, side), 1)
    row_gap = (
        lax.broadcasted_iota(jnp.int32, (PS, side), 0)
        - lax.broadcasted_iota(jnp.int32, (PS, side), 1)
    ).astype(F32).astype(BF16)
    one, zero = jnp.ones((), BF16), jnp.zeros((), BF16)
    lane = lax.broadcasted_iota(jnp.int32, (16, 128), 1)
    left_part = lane < side // 2

    def y_filter(t, s, d):
        c = [psf_ref[visit_ref[t], 9 * s + 3 * d + j] for j in range(3)]
        row = c[0] * g_ref[3 * s] + c[1] * g_ref[3 * s + 1] + c[2] * g_ref[3 * s + 2]
        row = row.astype(BF16)
        blocks = []
        for b in range(side // 16):
            block = pltpu.roll(row, (16 * b - HALF) % side, 1)
            if b == 0:
                block = jnp.where(left_part, block, zero)
            elif b == side // 16 - 1:
                block = jnp.where(left_part, zero, block)
            blocks.append(block)
        return jnp.concatenate(blocks, axis=0)

    def inside(t):
        return (row_of < extent_ref[0, t]) & (col_of < extent_ref[1, t])

    def smooth(i):
        stacked = []
        for t in (2 * i, 2 * i + 1):
            masked = jnp.where(inside(t), tiles_ref[t].astype(F32), 0.0).astype(BF16)
            wide = jnp.concatenate([y_filter(t, s, d) for s in range(3) for d in range(3)], axis=1)
            part = jnp.dot(masked, wide, preferred_element_type=F32).astype(BF16)
            stacked.append(
                jnp.concatenate([part[:, side * b:side * (b + 1)] for b in range(9)], axis=0)
            )
        return jnp.concatenate(stacked, axis=1)

    def finish(i, smoothed):
        convolved = jnp.dot(x_ref[...], smoothed, preferred_element_type=F32)
        for h in range(2):
            t = 2 * i + h
            scale = 1.0 / jnp.full((8, side), variance_ref[t], F32)
            matched[t] = jnp.where(
                inside(t), convolved[:, side * h:side * (h + 1)] * scale[0:1], 0.0
            ).astype(BF16)

    smoothed = smooth(0)
    for i in range(1, tile_count // 2):
        following = smooth(i)
        finish(i - 1, smoothed)
        smoothed = following
    finish(tile_count // 2 - 1, smoothed)

    def patch_sum(number):
        chosen, blocks = [], []
        for t in range(tile_count):
            first, second = inter_ref[0, t] == number, inter_ref[1, t] == number
            shift = jnp.where(
                first, offset_ref[0, 0, t], jnp.where(second, offset_ref[1, 0, t], 1024)
            )
            shift = jnp.full((PS, side), shift.astype(F32), F32).astype(BF16)
            chosen.append(jnp.where(row_gap == shift, one, zero))
            column = jnp.where(first, offset_ref[0, 1, t], offset_ref[1, 1, t])
            turned = pltpu.roll(matched[t], jnp.bitwise_and(column, side - 1), 1)
            gap = lane - column
            halves = []
            for low in (0, -side):
                mask = jnp.where((gap >= low) & (gap < low + side), 1.0, 0.0).astype(BF16)
                halves.append(turned * jnp.concatenate([mask] * (side // 16), axis=0))
            blocks.append(jnp.concatenate(halves, axis=1))
        return jnp.dot(
            jnp.concatenate(chosen, axis=1), jnp.concatenate(blocks, axis=0),
            preferred_element_type=F32,
        ).reshape(n_visit, rows, PS)

    def pair_copy(y):
        return pltpu.make_async_remote_copy(
            src_ref=away.at[y], dst_ref=from_pair.at[y],
            send_sem=pair_send, recv_sem=pair_recv.at[y],
            device_id=pair, device_id_type=MESH,
        )

    meta_copy = pltpu.make_async_remote_copy(
        src_ref=meta_own, dst_ref=meta_pair, send_sem=mp_send, recv_sem=mp_recv,
        device_id=pair, device_id_type=MESH,
    )

    def give(y):
        away[y] = patch_sum(2 * y + 1 - core).astype(BF16)

    def slot_of(dv, dy):
        return lax.rem(dy + n_y, n_y) * n_visit + lax.rem(dv + n_visit, n_visit)

    def meta_to(k):
        tv, ty = target(k)
        return pltpu.make_async_remote_copy(
            src_ref=meta_ready, dst_ref=meta_landed.at[k - 1],
            send_sem=msend_sem, recv_sem=mrecv_sem,
            device_id=(tv, 2 * ty + core), device_id_type=MESH,
        )

    def block_to(k):
        tv, ty = target(k)
        return pltpu.make_async_remote_copy(
            src_ref=ready.at[ty, tv], dst_ref=landed.at[k - 1],
            send_sem=send_sem, recv_sem=recv_sem,
            device_id=(tv, 2 * ty + core), device_id_type=MESH,
        )

    give(0)
    pl.semaphore_wait(barrier, slots)
    meta_copy.start()
    pair_copy(0).start()

    def give_next(y):
        give(y + 1)
        pair_copy(y + 1).start()

    repeat(n_y - 1, give_next)
    meta_copy.wait()
    meta_ready[...] = meta_own[...] + meta_pair[...]
    repeat(slots - 1, lambda i: meta_to(i + 1).start())

    def keep(y):
        total = patch_sum(2 * y + core)
        pair_copy(y).wait_recv()
        ready[y] = (total + from_pair[y].astype(F32)).astype(BF16)

    ORDER = sorted(
        [(tv, ty) for ty in range(n_y) for tv in range(n_visit)],
        key=lambda a: (a[0] // 2 + a[0] % 2 + a[1], a[1]),
    )
    own = sum(jnp.where((v == tv) & (chip_y == ty), j, 0) for j, (tv, ty) in enumerate(ORDER)) if slots <= 16 else 0

    def send(i):
        if slots <= 16:
            tv = jnp.where(i >= own, ORDER[i + 1][0], ORDER[i][0])
            ty = jnp.where(i >= own, ORDER[i + 1][1], ORDER[i][1])
            block_to(slot_of(tv - v, ty - chip_y)).start()
        else:
            block_to(i + 1).start()

    early = 2 if n_y == 2 else 0
    keep(0)
    repeat(early, send)
    repeat(n_y - 1, lambda y: keep(y + 1))
    repeat(slots - 1 - early, lambda i: send(i + early))

    canvas_row = (lax.broadcasted_iota(jnp.int32, (rows, 128), 0) + v * rows).astype(F32)
    canvas_col = lax.broadcasted_iota(jnp.int32, (PS, 128), 0).astype(F32)
    mine = p.astype(F32)
    first_half = entry < 64

    def weigh(one_chip, other_chip):
        spot = jnp.where(first_half, one_chip, pltpu.roll(other_chip, 64, 1))
        size = jnp.where(first_half, pltpu.roll(one_chip, 64, 1), other_chip)
        in_row = (canvas_row >= spot[1:2]) & (canvas_row < spot[1:2] + size[0:1])
        in_col = (canvas_col >= spot[2:3]) & (canvas_col < spot[2:3] + size[1:2])
        weight = jnp.where(spot[0:1] == mine, size[2:3], 0.0)
        coarse = weight.astype(BF16).astype(F32)
        both = lax.dot_general(
            jnp.concatenate(
                [jnp.where(in_row, coarse, 0.0), jnp.where(in_row, weight - coarse, 0.0)], axis=0
            ).astype(BF16),
            jnp.where(in_col, 1.0, 0.0).astype(BF16),
            (((1,), (1,)), ((), ())), preferred_element_type=F32,
        )
        return both[:rows] + both[rows:]

    def wait_all(landing, send, recv):
        pltpu.make_async_remote_copy(
            src_ref=landing, dst_ref=landing, send_sem=send, recv_sem=recv,
            device_id=pair, device_id_type=MESH,
        ).wait()

    wait_all(meta_landed, msend_sem, mrecv_sem)

    def add_meta(i, depth):
        return depth + weigh(meta_landed[2 * i - 1], meta_landed[2 * i])

    depth = weigh(meta_ready[...], meta_landed[0])
    if slots <= 16:
        for i in range(1, slots // 2):
            depth = add_meta(i, depth)
    else:
        depth = lax.fori_loop(1, slots // 2, add_meta, depth)
    depth_ref[...] = depth
    pltpu.make_async_remote_copy(
        src_ref=away, dst_ref=from_pair, send_sem=pair_send, recv_sem=pair_recv.at[0],
        device_id=pair, device_id_type=MESH,
    ).wait_send()
    wait_all(landed, send_sem, recv_sem)

    def add_block(i, total):
        return total + landed[i].astype(F32)

    total = ready[chip_y, v].astype(F32)
    if slots <= 16:
        for i in range(slots - 1):
            total = add_block(i, total)
    else:
        total = lax.fori_loop(0, slots - 1, add_block, total)
    flux_ref[...] = total


def solution(mesh):
    n_visit, n_patch = mesh.shape["visit"], mesh.shape["patch"]

    def body(tiles, tile_visit, tile_variance, intersection, offsets, extent, psf_coeffs):
        tile_count, side = tiles.shape[0], tiles.shape[1]
        rows = PS // n_visit
        n_y = n_patch // 2
        slots = n_visit * n_y
        x_filter, stagger = filters(side)
        anywhere = pl.BlockSpec(memory_space=pl.ANY)
        arrays = (
            tile_visit, tile_variance, intersection.T, jnp.transpose(offsets, (1, 2, 0)), extent.T,
            psf_coeffs, tiles, jnp.asarray(x_filter, BF16), jnp.asarray(stagger, F32),
        )
        vmem = pl.BlockSpec(memory_space=pltpu.VMEM)
        dma = pltpu.SemaphoreType.DMA
        flux, depth = pl.pallas_call(
            functools.partial(kernel, (n_visit, n_patch, tile_count, side)),
            out_shape=[pltpu.VMEM((rows, PS), F32)] * 2,
            in_specs=[anywhere] * 9,
            out_specs=[vmem] * 2,
            scratch_shapes=[pltpu.SMEM(a.shape, a.dtype) for a in arrays[:6]]
            + [pltpu.VMEM(a.shape, a.dtype) for a in arrays[6:]]
            + [
                dma((9,)),
                pltpu.VMEM((tile_count, side, side), BF16),
                pltpu.VMEM((n_y, n_visit, rows, PS), BF16),
                pltpu.VMEM((n_y, n_visit, rows, PS), BF16),
                pltpu.VMEM((n_y, n_visit, rows, PS), BF16),
                pltpu.VMEM((slots - 1, rows, PS), BF16),
                pltpu.VMEM((4, 128), F32),
                pltpu.VMEM((4, 128), F32),
                pltpu.VMEM((4, 128), F32),
                pltpu.VMEM((slots - 1, 4, 128), F32),
                dma, dma((n_y,)), dma, dma, dma, dma, dma, dma,
            ],
            compiler_params=pltpu.CompilerParams(
                collective_id=0, has_side_effects=True, vmem_limit_bytes=62 * 2**20
            ),
        )(*[pltpu.with_memory_space_constraint(a, pltpu.HBM) for a in arrays])
        return (flux / jnp.sqrt(depth + 1.0))[None]

    return jax.shard_map(
        body,
        mesh=mesh,
        in_specs=(
            P(("visit", "patch"), None, None),
            P(("visit", "patch")),
            P(("visit", "patch")),
            P(("visit", "patch"), None),
            P(("visit", "patch"), None, None),
            P(("visit", "patch"), None),
            P("visit", None),
        ),
        out_specs=P("patch", "visit", None),
        check_vma=False,
    )
```

```python
import functools
import math

import jax
import jax.numpy as jnp
import numpy as np
from jax import lax
from jax.experimental import pallas as pl
from jax.experimental.pallas import tpu as pltpu
from jax.sharding import PartitionSpec as P

PS = 256
HALF = 10
SIGMAS = (0.7, 1.5, 3.0)
MESH = pl.DeviceIdType.MESH
F32, BF16 = jnp.float32, jnp.bfloat16


def taps():
    lag = np.arange(-HALF, HALF + 1, dtype=np.float32)
    rows = []
    for sigma in SIGMAS:
        scaled = (lag / np.float32(sigma)).astype(np.float32)
        gaussian = np.exp(np.float32(-0.5) * scaled * scaled) / np.float32(
            math.sqrt(2.0 * math.pi) * sigma
        )
        rows += [gaussian, scaled * gaussian, scaled * scaled * gaussian]
    return np.stack(rows).astype(np.float32)


def filters(side):
    pixel = np.arange(side)
    lag = pixel[:, None] - pixel[None, :]
    banded = np.where(
        np.abs(lag) <= HALF, taps()[:, np.clip(lag, -HALF, HALF) + HALF], np.float32(0)
    )
    x_filter = np.concatenate(list(banded), axis=1)
    stagger = np.zeros((9, 16, side), np.float32)
    for i in range(16):
        stagger[:, i, i:i + 2 * HALF + 1] = taps()
    return x_filter, stagger


def repeat(count, step):
    if count <= 16:
        for i in range(count):
            step(i)
    else:
        def body(i, carry):
            step(i)
            return carry

        lax.fori_loop(0, count, body, 0)


def kernel(dims, *refs):
    inputs, (flux_ref, depth_ref), held, rest = refs[:9], refs[9:11], refs[11:20], refs[20:]
    work(dims, inputs, held, flux_ref, depth_ref, *rest)


def work(
    dims, inputs, held, flux_ref, depth_ref, load_sem,
    matched, kept, away, from_pair, ready, landed, meta_own, meta_pair, meta_ready, meta_landed,
    pair_send, pair_recv, mp_send, mp_recv, send_sem, recv_sem, msend_sem, mrecv_sem,
):
    n_visit, n_patch, tile_count, side = dims
    visit_ref, variance_ref, inter_ref, offset_ref, extent_ref, psf_ref, tiles_ref, x_ref, g_ref = held
    loads = [pltpu.make_async_copy(a, b, load_sem.at[i]) for i, (a, b) in enumerate(zip(inputs, held))]
    for load in loads:
        load.start()
    n_y = n_patch // 2
    rows = PS // n_visit
    slots = n_visit * n_y
    v = lax.axis_index("visit")
    p = lax.axis_index("patch")
    core = lax.rem(p, 2)
    chip_y = lax.div(p, 2)
    pair = (v, p + 1 - 2 * core)

    def target(k):
        return (lax.rem(v + lax.rem(k, n_visit), n_visit), lax.rem(chip_y + lax.div(k, n_visit), n_y))

    barrier = pltpu.get_barrier_semaphore()
    pl.semaphore_signal(barrier, inc=1, device_id=pair, device_id_type=MESH)

    def greet(k, carry):
        tv, ty = target(k)
        pl.semaphore_signal(barrier, inc=1, device_id=(tv, 2 * ty + core), device_id_type=MESH)
        return carry

    lax.fori_loop(1, slots, greet, 0)
    for load in loads:
        load.wait()

    field = lax.broadcasted_iota(jnp.int32, (4, 128), 0)
    entry = lax.broadcasted_iota(jnp.int32, (4, 128), 1)
    table = jnp.zeros((4, 128), F32)
    at = 2 * tile_count * core
    for t in range(tile_count):
        size = jnp.where(
            field == 0, extent_ref[0, t].astype(F32),
            jnp.where(field == 1, extent_ref[1, t].astype(F32), variance_ref[t]),
        )
        for k in range(2):
            spot = jnp.where(
                field == 0, inter_ref[k, t].astype(F32),
                jnp.where(field == 1, offset_ref[k, 0, t].astype(F32), offset_ref[k, 1, t].astype(F32)),
            )
            table = jnp.where(entry == at + 2 * t + k, spot, table)
            table = jnp.where(entry == at + 64 + 2 * t + k, size, table)
    own_size = (field == 2) & (entry >= at + 64) & (entry < at + 64 + 2 * tile_count)
    meta_own[...] = jnp.where(own_size, 1.0 / jnp.where(own_size, table, 1.0), table)

    row_of = lax.broadcasted_iota(jnp.int32, (side, side), 0)
    col_of = lax.broadcasted_iota(jnp.int32, (side, side), 1)
    row_gap = (
        lax.broadcasted_iota(jnp.int32, (PS, side), 0)
        - lax.broadcasted_iota(jnp.int32, (PS, side), 1)
    ).astype(F32).astype(BF16)
    one, zero = jnp.ones((), BF16), jnp.zeros((), BF16)
    lane = lax.broadcasted_iota(jnp.int32, (16, 128), 1)
    left_part = lane < side // 2

    def y_filter(t, s, d):
        c = [psf_ref[visit_ref[t], 9 * s + 3 * d + j] for j in range(3)]
        row = c[0] * g_ref[3 * s] + c[1] * g_ref[3 * s + 1] + c[2] * g_ref[3 * s + 2]
        row = row.astype(BF16)
        blocks = []
        for b in range(side // 16):
            block = pltpu.roll(row, (16 * b - HALF) % side, 1)
            if b == 0:
                block = jnp.where(left_part, block, zero)
            elif b == side // 16 - 1:
                block = jnp.where(left_part, zero, block)
            blocks.append(block)
        return jnp.concatenate(blocks, axis=0)

    def inside(t):
        return (row_of < extent_ref[0, t]) & (col_of < extent_ref[1, t])

    def smooth(i):
        stacked = []
        for t in (2 * i, 2 * i + 1):
            masked = jnp.where(inside(t), tiles_ref[t].astype(F32), 0.0).astype(BF16)
            wide = jnp.concatenate([y_filter(t, s, d) for s in range(3) for d in range(3)], axis=1)
            part = jnp.dot(masked, wide, preferred_element_type=F32).astype(BF16)
            stacked.append(
                jnp.concatenate([part[:, side * b:side * (b + 1)] for b in range(9)], axis=0)
            )
        return jnp.concatenate(stacked, axis=1)

    def finish(i, smoothed):
        convolved = jnp.dot(x_ref[...], smoothed, preferred_element_type=F32)
        for h in range(2):
            t = 2 * i + h
            scale = 1.0 / jnp.full((8, side), variance_ref[t], F32)
            matched[t] = jnp.where(
                inside(t), convolved[:, side * h:side * (h + 1)] * scale[0:1], 0.0
            ).astype(BF16)

    smoothed = smooth(0)
    for i in range(1, tile_count // 2):
        following = smooth(i)
        finish(i - 1, smoothed)
        smoothed = following
    finish(tile_count // 2 - 1, smoothed)

    def patch_sum(number):
        chosen, blocks = [], []
        for t in range(tile_count):
            first, second = inter_ref[0, t] == number, inter_ref[1, t] == number
            shift = jnp.where(
                first, offset_ref[0, 0, t], jnp.where(second, offset_ref[1, 0, t], 1024)
            )
            shift = jnp.full((PS, side), shift.astype(F32), F32).astype(BF16)
            chosen.append(jnp.where(row_gap == shift, one, zero))
            column = jnp.where(first, offset_ref[0, 1, t], offset_ref[1, 1, t])
            turned = pltpu.roll(matched[t], jnp.bitwise_and(column, side - 1), 1)
            gap = lane - column
            halves = []
            for low in (0, -side):
                mask = jnp.where((gap >= low) & (gap < low + side), 1.0, 0.0).astype(BF16)
                halves.append(turned * jnp.concatenate([mask] * (side // 16), axis=0))
            blocks.append(jnp.concatenate(halves, axis=1))
        return jnp.dot(
            jnp.concatenate(chosen, axis=1), jnp.concatenate(blocks, axis=0),
            preferred_element_type=F32,
        ).reshape(n_visit, rows, PS)

    def pair_copy(y):
        return pltpu.make_async_remote_copy(
            src_ref=away.at[y], dst_ref=from_pair.at[y],
            send_sem=pair_send, recv_sem=pair_recv.at[y],
            device_id=pair, device_id_type=MESH,
        )

    meta_copy = pltpu.make_async_remote_copy(
        src_ref=meta_own, dst_ref=meta_pair, send_sem=mp_send, recv_sem=mp_recv,
        device_id=pair, device_id_type=MESH,
    )

    def give(y):
        away[y] = patch_sum(2 * y + 1 - core).astype(BF16)

    def slot_of(dv, dy):
        return lax.rem(dy + n_y, n_y) * n_visit + lax.rem(dv + n_visit, n_visit)

    def meta_to(k):
        tv, ty = target(k)
        return pltpu.make_async_remote_copy(
            src_ref=meta_ready, dst_ref=meta_landed.at[k - 1],
            send_sem=msend_sem, recv_sem=mrecv_sem,
            device_id=(tv, 2 * ty + core), device_id_type=MESH,
        )

    def block_to(k):
        tv, ty = target(k)
        return pltpu.make_async_remote_copy(
            src_ref=ready.at[ty, tv], dst_ref=landed.at[k - 1],
            send_sem=send_sem, recv_sem=recv_sem,
            device_id=(tv, 2 * ty + core), device_id_type=MESH,
        )

    order = [(tv, ty) for tv in range(n_visit) for ty in range(n_y)]
    if slots <= 16:
        order.sort(key=lambda d: (d[0] // 2 + d[0] % 2 + d[1], d[1]))
    own = sum(jnp.where((v == tv) & (chip_y == ty), j, 0) for j, (tv, ty) in enumerate(order)) \
        if slots <= 16 else v * n_y + chip_y

    def send(i):
        j = i + jnp.where(i >= own, 1, 0)
        if slots <= 16:
            tv = jnp.where(i >= own, order[i + 1][0], order[i][0])
            ty = jnp.where(i >= own, order[i + 1][1], order[i][1])
        else:
            tv, ty = lax.div(j, n_y), lax.rem(j, n_y)
        block_to(slot_of(tv - v, ty - chip_y)).start()

    pl.semaphore_wait(barrier, slots)
    meta_copy.start()
    give(0)
    pair_copy(0).start()

    def give_next(y):
        give(y + 1)
        pair_copy(y + 1).start()

    repeat(n_y - 1, give_next)

    def hold(y):
        kept[y] = patch_sum(2 * y + core)

    def keep(y):
        pair_copy(y).wait_recv()
        ready[y] = (kept[y] + from_pair[y].astype(F32)).astype(BF16)

    meta_copy.wait()
    meta_ready[...] = meta_own[...] + meta_pair[...]
    repeat(slots - 1, lambda i: meta_to(i + 1).start())
    hold(0)

    @pl.when(core == 1)
    def _():
        repeat(n_y - 1, lambda y: hold(y + 1))

    keep(0)
    early = 2 if n_y == 2 else 0
    repeat(early, send)

    @pl.when(core == 0)
    def _():
        repeat(n_y - 1, lambda y: hold(y + 1))

    repeat(n_y - 1, lambda y: keep(y + 1))
    repeat(slots - 1 - early, lambda i: send(i + early))

    canvas_row = (lax.broadcasted_iota(jnp.int32, (rows, 128), 0) + v * rows).astype(F32)
    canvas_col = lax.broadcasted_iota(jnp.int32, (PS, 128), 0).astype(F32)
    mine = p.astype(F32)
    first_half = entry < 64

    def weigh(one_chip, other_chip):
        spot = jnp.where(first_half, one_chip, pltpu.roll(other_chip, 64, 1))
        size = jnp.where(first_half, pltpu.roll(one_chip, 64, 1), other_chip)
        in_row = (canvas_row >= spot[1:2]) & (canvas_row < spot[1:2] + size[0:1])
        in_col = (canvas_col >= spot[2:3]) & (canvas_col < spot[2:3] + size[1:2])
        weight = jnp.where(spot[0:1] == mine, size[2:3], 0.0)
        coarse = weight.astype(BF16).astype(F32)
        both = lax.dot_general(
            jnp.concatenate(
                [jnp.where(in_row, coarse, 0.0), jnp.where(in_row, weight - coarse, 0.0)], axis=0
            ).astype(BF16),
            jnp.where(in_col, 1.0, 0.0).astype(BF16),
            (((1,), (1,)), ((), ())), preferred_element_type=F32,
        )
        return both[:rows] + both[rows:]

    def wait_all(landing, send, recv):
        pltpu.make_async_remote_copy(
            src_ref=landing, dst_ref=landing, send_sem=send, recv_sem=recv,
            device_id=pair, device_id_type=MESH,
        ).wait()

    wait_all(meta_landed, msend_sem, mrecv_sem)

    def add_meta(i, depth):
        return depth + weigh(meta_landed[2 * i - 1], meta_landed[2 * i])

    depth = weigh(meta_ready[...], meta_landed[0])
    if slots <= 16:
        for i in range(1, slots // 2):
            depth = add_meta(i, depth)
    else:
        depth = lax.fori_loop(1, slots // 2, add_meta, depth)
    depth_ref[...] = depth
    pltpu.make_async_remote_copy(
        src_ref=away, dst_ref=from_pair, send_sem=pair_send, recv_sem=pair_recv.at[0],
        device_id=pair, device_id_type=MESH,
    ).wait_send()
    wait_all(landed, send_sem, recv_sem)

    def add_block(i, total):
        return total + landed[i].astype(F32)

    total = ready[chip_y, v].astype(F32)
    if slots <= 16:
        for i in range(slots - 1):
            total = add_block(i, total)
    else:
        total = lax.fori_loop(0, slots - 1, add_block, total)
    flux_ref[...] = total


def solution(mesh):
    n_visit, n_patch = mesh.shape["visit"], mesh.shape["patch"]

    def body(tiles, tile_visit, tile_variance, intersection, offsets, extent, psf_coeffs):
        tile_count, side = tiles.shape[0], tiles.shape[1]
        rows = PS // n_visit
        n_y = n_patch // 2
        slots = n_visit * n_y
        x_filter, stagger = filters(side)
        anywhere = pl.BlockSpec(memory_space=pl.ANY)
        arrays = (
            tile_visit, tile_variance, intersection.T, jnp.transpose(offsets, (1, 2, 0)), extent.T,
            psf_coeffs, tiles, jnp.asarray(x_filter, BF16), jnp.asarray(stagger, F32),
        )
        vmem = pl.BlockSpec(memory_space=pltpu.VMEM)
        dma = pltpu.SemaphoreType.DMA
        flux, depth = pl.pallas_call(
            functools.partial(kernel, (n_visit, n_patch, tile_count, side)),
            out_shape=[pltpu.VMEM((rows, PS), F32)] * 2,
            in_specs=[anywhere] * 9,
            out_specs=[vmem] * 2,
            scratch_shapes=[pltpu.SMEM(a.shape, a.dtype) for a in arrays[:6]]
            + [pltpu.VMEM(a.shape, a.dtype) for a in arrays[6:]]
            + [
                dma((9,)),
                pltpu.VMEM((tile_count, side, side), BF16),
                pltpu.VMEM((n_y, n_visit, rows, PS), F32),
                pltpu.VMEM((n_y, n_visit, rows, PS), BF16),
                pltpu.VMEM((n_y, n_visit, rows, PS), BF16),
                pltpu.VMEM((n_y, n_visit, rows, PS), BF16),
                pltpu.VMEM((slots - 1, rows, PS), BF16),
                pltpu.VMEM((4, 128), F32),
                pltpu.VMEM((4, 128), F32),
                pltpu.VMEM((4, 128), F32),
                pltpu.VMEM((slots - 1, 4, 128), F32),
                dma, dma((n_y,)), dma, dma, dma, dma, dma, dma,
            ],
            compiler_params=pltpu.CompilerParams(
                collective_id=0, has_side_effects=True, vmem_limit_bytes=62 * 2**20
            ),
        )(*[pltpu.with_memory_space_constraint(a, pltpu.HBM) for a in arrays])
        return (flux / jnp.sqrt(depth + 1.0))[None]

    return jax.shard_map(
        body,
        mesh=mesh,
        in_specs=(
            P(("visit", "patch"), None, None),
            P(("visit", "patch")),
            P(("visit", "patch")),
            P(("visit", "patch"), None),
            P(("visit", "patch"), None, None),
            P(("visit", "patch"), None),
            P("visit", None),
        ),
        out_specs=P("patch", "visit", None),
        check_vma=False,
    )
```
